32 devices in a mesh: mpo: 4 (over x, core), bond: 8 (over z, y).
Axes of the slice: x: 2, y: 2, z: 4, core: 2. Of those that a mesh axis runs over, the one named last changes fastest.
Arguments:
- environment: bfloat16 [4096, 40, 4096], P(None, 'mpo', 'bond'), may hold values from -60 to 60
- site_tensor: bfloat16 [4096, 4, 4096], P('bond'), may hold values from -0.09375 to 0.09375
- mpo_tensor: bfloat16 [40, 40, 4, 4], replicated, may hold values from -0.5 to 0.5
- sketch_site: bfloat16 [4096, 128], replicated, may hold values from -6 to 6
- sketch_expand: bfloat16 [128, 40, 4096], P('mpo'), may hold values from -60 to 60
- row_sectors: int32 [2, 4096, 4], P(None, 'bond'), may hold values from 0 to 5, as said below
- column_sectors: int32 [2, 128], replicated, may hold values from 0 to 5, as said below
Outputs:
- basis: bfloat16 [4096, 4, 128], P('bond')
- extended: float32 [128, 40, 128], P('bond', 'mpo')
The draws below stay inside these ranges and needn't reach their ends.
Inputs may be any that keep to these rules, and one draw needn't show every extreme that they name: `row_sectors`: every joined row's label pair is (4, 0) or (5, 1); the rows labelled (5, 1) are one run of 64 consecutive joined rows (a, s) in the order a then s. `column_sectors`: every column's label pair is (4, 0) or (5, 1); exactly 16 columns are labelled (5, 1).
All inputs are finite; a program needn't handle non-finite values.
Results may differ from the reference program's by a relative error of at most 0.0064.
Values may be sent and summed in bfloat16 or wider, within the bound.
A program may use at most 128 MiB of HBM per device.

```python
import math
import jax
import jax.numpy as jnp
from jax import lax

CHI = 4096
W = 40
D = 4
K = 128


def draw_environment(key, part):
    base_key, scale_key = jax.random.split(jax.random.fold_in(key, 11))
    base = jnp.clip(jax.random.normal(base_key, (CHI, W, CHI), jnp.float32), -6.0, 6.0)
    scale = jnp.exp(jax.random.uniform(scale_key, (CHI, 1, 1), jnp.float32, 0.0, math.log(10.0)))
    return (base * scale).astype(jnp.bfloat16)


def draw_sketch_expand(key, part):
    base_key, scale_key = jax.random.split(jax.random.fold_in(key, 23))
    base = jnp.clip(jax.random.normal(base_key, (K, W, CHI), jnp.float32), -6.0, 6.0)
    scale = jnp.exp(jax.random.uniform(scale_key, (K, 1, 1), jnp.float32, 0.0, math.log(10.0)))
    return (base * scale).astype(jnp.bfloat16)


def draw_row_sectors(key, part):
    run_length = K // 2
    start = jax.random.randint(jax.random.fold_in(key, 31), (), 0, CHI * D - run_length + 1, dtype=jnp.int32)
    position = jnp.arange(CHI * D, dtype=jnp.int32)
    choose = ((position >= start) & (position < start + run_length)).astype(jnp.int32)
    return jnp.stack([4 + choose, choose]).reshape(2, CHI, D)


def draw_column_sectors(key, part):
    order = jax.random.permutation(jax.random.fold_in(key, 37), K)
    choose = (order < K // 8).astype(jnp.int32)
    return jnp.stack([4 + choose, choose])


def level_of(key, dims, shards, smallest, high):
    loudness, own = 1.0, jax.random.fold_in(key, 6)
    for dim, blocks in shards:
        draws = jnp.exp(jax.random.uniform(jax.random.fold_in(own, dim), (blocks,), jnp.float32, smallest / len(shards), high / len(shards)))
        loudness = loudness * jnp.repeat(draws, dims[dim] // blocks).reshape([-1 if axis == dim else 1 for axis in range(len(dims))])
    return loudness


def scatter_about(key, shape, deviation, limit, cuts=(), kind=jnp.bfloat16):
    values = deviation * jax.random.normal(key, shape, jnp.float32)
    if cuts:
        values = values * level_of(key, shape, cuts, -0.22, 0.18)
    return jnp.clip(values, -limit, limit).astype(kind)


def setup_inputs(seed: int = 0) -> dict:
    streams_of = jax.random.split(jax.random.key(seed), 8)
    environment = draw_environment(jax.random.fold_in(streams_of[7], 71), 0)
    site_tensor = scatter_about(streams_of[1], (CHI, D, CHI), CHI ** -0.5, 0.09375, ((0, 8),))
    mpo_tensor = scatter_about(streams_of[2], (W, W, D, D), (W * D) ** -0.5, 0.5)
    sketch_site = scatter_about(streams_of[3], (CHI, K), 1.0, 6.0)
    sketch_expand = draw_sketch_expand(jax.random.fold_in(streams_of[7], 71), 0)
    row_sectors = draw_row_sectors(jax.random.fold_in(streams_of[7], 71), 0)
    column_sectors = draw_column_sectors(jax.random.fold_in(streams_of[7], 71), 0)
    return dict(environment=environment, site_tensor=site_tensor, mpo_tensor=mpo_tensor, sketch_site=sketch_site, sketch_expand=sketch_expand, row_sectors=row_sectors, column_sectors=column_sectors)


mixing = 0.5
shift_tolerance = 1e-06

def sector_mask(row_labels, column_labels):
    match = (row_labels[0][:, :, None] == column_labels[0][None, None, :]) & (row_labels[1][:, :, None] == column_labels[1][None, None, :])
    return match.astype(jnp.float32)

def reference(environment, site_tensor, mpo_tensor, sketch_site, sketch_expand, row_sectors, column_sectors):
    highest_accuracy = lax.Precision.HIGHEST
    site_flat = site_tensor.reshape(CHI * D, CHI).astype(jnp.float32)
    indices = jnp.arange(W, dtype=jnp.int32)

    def sketch_one(index):
        random_probe_matrix = lax.dynamic_index_in_dim(sketch_expand, index, 1, keepdims=False).astype(jnp.float32)
        block = jnp.dot(site_flat, random_probe_matrix.T, precision=highest_accuracy)
        return jnp.transpose(block.reshape(CHI, D, K), (1, 2, 0)).astype(jnp.bfloat16)
    sketched = lax.map(sketch_one, indices)
    contracted = jnp.einsum('vwst,wtka->vska', mpo_tensor.astype(jnp.float32), sketched.astype(jnp.float32), precision=highest_accuracy).astype(jnp.bfloat16)

    def expand_one(index):
        env_w = lax.dynamic_index_in_dim(environment, index, 1, keepdims=False).astype(jnp.float32)
        part_w = lax.dynamic_index_in_dim(contracted, index, 0, keepdims=False).astype(jnp.float32).reshape(D * K, CHI)
        return jnp.dot(env_w, part_w.T, precision=highest_accuracy)
    enlarged_range = lax.optimization_barrier(jnp.sum(lax.map(expand_one, indices), axis=0)).reshape(CHI, D, K)
    site_y = jnp.dot(site_tensor.reshape(CHI * D, CHI).astype(jnp.float32), sketch_site.astype(jnp.float32), preferred_element_type=jnp.float32).reshape(CHI, D, K)
    mask = sector_mask(row_sectors, column_sectors)
    masked_site = site_y * mask
    filtered_enlarged = enlarged_range * mask
    mix = mixing * jnp.sqrt((jnp.sum(masked_site * masked_site) + shift_tolerance) / (jnp.sum(filtered_enlarged * filtered_enlarged) + shift_tolerance))
    combined = (masked_site + mix * filtered_enlarged).reshape(CHI * D, K)
    gram = jnp.dot(combined.T.astype(jnp.float32), combined.astype(jnp.float32), precision=highest_accuracy, preferred_element_type=jnp.float32)
    factor = jnp.linalg.cholesky(gram)
    solved = jax.scipy.linalg.solve_triangular(factor, combined.T, lower=True)
    basis = solved.T.reshape(CHI, D, K).astype(jnp.bfloat16)
    basis_flat = basis.reshape(CHI, D * K).astype(jnp.float32)

    def project_one(index):
        env_w = lax.dynamic_index_in_dim(environment, index, 1, keepdims=False).astype(jnp.float32)
        return jnp.dot(basis_flat.T, env_w, precision=highest_accuracy).astype(jnp.bfloat16)
    projected = lax.map(project_one, indices)

    def extend_one(index):
        proj_w = lax.dynamic_index_in_dim(projected, index, 0, keepdims=False).astype(jnp.float32)
        couple_merged = jnp.dot(proj_w, basis_flat, precision=highest_accuracy).reshape(D, K, D, K)
        hamiltonian_factor = lax.dynamic_index_in_dim(mpo_tensor, index, 0, keepdims=False).astype(jnp.float32)
        return jnp.einsum('uod,oydq->yuq', hamiltonian_factor, couple_merged, precision=highest_accuracy)
    extended = lax.optimization_barrier(jnp.sum(lax.map(extend_one, indices), axis=0))
    return (basis, extended)
```

```python
import jax
import jax.numpy as jnp
from jax import lax
from jax.experimental.layout import Layout, with_layout_constraint
from jax.sharding import PartitionSpec as P


mixing = 0.5
shift_tolerance = 1e-06


def bits_of(size):
    return size.bit_length() - 1


def axis_bits(axis):
    return [(axis, bit) for bit in reversed(range(bits_of(lax.axis_size(axis))))]


def exchange(value, step):
    axis, bit = step
    pairs = [(i, i ^ (1 << bit)) for i in range(lax.axis_size(axis))]
    return lax.ppermute(value, axis, pairs)


def own_bit(step):
    axis, bit = step
    return (lax.axis_index(axis) >> bit) & 1


def row_major(value):
    return with_layout_constraint(value, Layout(major_to_minor=tuple(range(value.ndim))))


def scatter_sum(value, dims, order, narrow=()):
    dims = list(dims)
    for step in order:
        place = dims.index(step)
        mine = own_bit(step)
        send = lax.dynamic_index_in_dim(value, 1 - mine, place, keepdims=False)
        keep = lax.dynamic_index_in_dim(value, mine, place, keepdims=False)
        if step in narrow:
            send = send.astype(jnp.bfloat16)
        other = exchange(send, step)
        value = keep + other.astype(jnp.float32)
        dims.pop(place)
    return value


def gather(value, dims, order):
    held = []
    for step in order:
        place = sum(dims.index(other) < dims.index(step) for other in held)
        other = exchange(value, step)
        mine = own_bit(step)
        value = jnp.where(
            mine == 0,
            jnp.stack([value, other], place),
            jnp.stack([other, value], place),
        )
        held.append(step)
    return value


def total_over_all(value, split, rest):
    shape = value.shape
    value = value.reshape((2,) * len(split) + (-1, shape[-1]))
    value = scatter_sum(value, split, list(reversed(split)))
    for step in rest:
        value = value + exchange(value, step)
    value = gather(value, split, split)
    return value.reshape(shape)


def body(
    environment, site_tensor, mpo_tensor, sketch_site, sketch_expand, row_sectors, column_sectors
):
    me = lax.axis_index("mpo")
    bond_me = lax.axis_index("bond")
    mpo_count = lax.axis_size("mpo")
    bond_count = lax.axis_size("bond")
    physical_width = environment.shape[1]
    local_rows, physical, _ = site_tensor.shape
    own_columns, mpo_width, _ = sketch_expand.shape
    column_count = column_sectors.shape[1]
    total_rows = environment.shape[0]
    share = local_rows // mpo_count
    mpo_bits, bond_bits = axis_bits("mpo"), axis_bits("bond")
    all_bits = bond_bits + mpo_bits
    core, chips_x = mpo_bits[-1:], list(reversed(mpo_bits[:-1]))
    along_bond = list(reversed(bond_bits))
    chunks = 2
    part = own_columns // chunks

    site_major = lax.optimization_barrier(row_major(jnp.swapaxes(site_tensor, 0, 1)))
    operator = mpo_tensor.reshape(mpo_count, physical_width, mpo_width, physical, physical)
    operator = jnp.stack(
        [lax.dynamic_index_in_dim(operator, me ^ d, 0, keepdims=False) for d in range(mpo_count)]
    )
    traded = []
    for chunk in range(chunks):
        sketched = jnp.einsum(
            "sab,kwb->wska",
            site_major,
            sketch_expand[chunk * part : (chunk + 1) * part],
            preferred_element_type=jnp.float32,
        ).astype(jnp.bfloat16)
        applied = jnp.einsum(
            "dvwst,wtka->dvska", operator, sketched, preferred_element_type=jnp.float32
        ).astype(jnp.bfloat16)
        blocks = [applied[0]]
        for d in range(1, mpo_count):
            blocks.append(lax.ppermute(applied[d], "mpo", [(i, i ^ d) for i in range(mpo_count)]))
        traded.append(blocks)

    orders = [core + along_bond + chips_x, core + chips_x + along_bond]
    pieces = []
    partial = None
    for chunk in range(chunks):
        blocks = traded[chunk]
        if chunk:
            blocks, partial = lax.optimization_barrier((blocks, partial))
        held = jnp.zeros(
            (physical_width, physical, mpo_count, part, local_rows), jnp.bfloat16
        )
        for d in range(mpo_count):
            held = lax.dynamic_update_slice_in_dim(held, blocks[d][:, :, None], me ^ d, 2)
        partial = jnp.einsum(
            "awc,wnc->an",
            environment,
            held.reshape(physical_width, -1, local_rows),
            preferred_element_type=jnp.float32,
        )
        partial = row_major(partial)
        pieces.append((partial, orders[chunk]))
    pieces = [
        scatter_sum(
            value.reshape((2,) * len(all_bits) + (share, -1)), all_bits, order, all_bits
        ).reshape(share, physical, mpo_count, part)
        for value, order in pieces
    ]
    expand_y = jnp.stack(pieces, 3).reshape(share, physical, column_count)

    own_rows = lax.dynamic_slice_in_dim(site_major, me * share, share, 1)
    site_y = jnp.einsum(
        "sab,bk->ask", own_rows, sketch_site, preferred_element_type=jnp.float32
    )
    labels = lax.dynamic_slice_in_dim(row_sectors, me * share, share, 1)
    mask = (
        (labels[0][:, :, None] == column_sectors[0][None, None, :])
        & (labels[1][:, :, None] == column_sectors[1][None, None, :])
    ).astype(jnp.float32)
    site_flat = (site_y * mask).reshape(-1, column_count)
    expand_flat = (expand_y * mask).reshape(-1, column_count)

    def product(left, right):
        return jnp.dot(
            left.T, right, precision=lax.Precision.HIGHEST, preferred_element_type=jnp.float32
        )

    cross = product(site_flat, expand_flat)
    grams = jnp.concatenate(
        [product(site_flat, site_flat), cross + cross.T, product(expand_flat, expand_flat)]
    )
    grams = total_over_all(grams, mpo_bits, along_bond).reshape(3, column_count, column_count)
    square_site, square_expand = jnp.trace(grams[0]), jnp.trace(grams[2])
    mix = mixing * jnp.sqrt((square_site + shift_tolerance) / (square_expand + shift_tolerance))
    factor = jnp.linalg.cholesky(grams[0] + mix * grams[1] + (mix * mix) * grams[2])
    combined = site_flat + mix * expand_flat
    solved = jax.scipy.linalg.solve_triangular(factor, combined.T, lower=True)
    basis_piece = solved.T.reshape(share, -1).astype(jnp.bfloat16)

    halves = 2
    width = basis_piece.shape[1] // halves
    order = bond_bits + mpo_bits
    whole = []
    for half in range(halves):
        piece = basis_piece[:, half * width : (half + 1) * width]
        item = gather(piece, all_bits, order)
        whole.append(row_major(item.reshape(total_rows, width)))
    own_basis = jnp.concatenate(
        [lax.dynamic_slice_in_dim(item, bond_me * local_rows, local_rows, 0) for item in whole], 1
    )
    operator_rows = lax.dynamic_slice_in_dim(
        mpo_tensor, me * physical_width, physical_width, 0
    )
    own_basis = own_basis.reshape(local_rows, physical, column_count)
    per = physical // halves
    extended = 0.0
    for half in range(halves):
        projected = jnp.einsum(
            "ax,awc->wxc", whole[half], environment, preferred_element_type=jnp.float32
        ).astype(jnp.bfloat16)
        paired = jnp.einsum(
            "wskc,ctl->wsktl",
            projected.reshape(physical_width, per, column_count, local_rows),
            own_basis,
            preferred_element_type=jnp.float32,
        ).astype(jnp.bfloat16)
        extended = extended + jnp.einsum(
            "wvst,wsktl->vkl",
            operator_rows[:, :, half * per : (half + 1) * per],
            paired,
            preferred_element_type=jnp.float32,
        )
    extended = row_major(extended).reshape(
        (2,) * len(mpo_bits)
        + (mpo_width // mpo_count,)
        + (2,) * len(bond_bits)
        + (column_count // bond_count, column_count)
    )
    extended = scatter_sum(
        extended,
        mpo_bits + [None] + bond_bits,
        core + chips_x + along_bond,
        chips_x + along_bond,
    )
    return own_basis, jnp.swapaxes(extended, 0, 1)


def solution(mesh):
    placed = (
        P(None, "mpo", "bond"),
        P("bond", None, None),
        P(),
        P(),
        P("mpo", None, None),
        P(None, "bond", None),
        P(),
    )

    return jax.shard_map(
        body,
        mesh=mesh,
        in_specs=placed,
        out_specs=(P("bond", None, None), P("bond", "mpo", None)),
        check_vma=False,
    )
```
